32 devices in a mesh: dp: 8 (over z, x), tensor: 4 (over y, core).
Axes of the slice: x: 2, y: 2, z: 4, core: 2. Of those that a mesh axis runs over, the one named last changes fastest.
Arguments:
- tokens: bfloat16 [4096, 2048], P(('dp', 'tensor')), may hold values from -6 to 6
- lengths: int32 [8], P('dp'), may hold values from 256 to 512, as said below
- w_query: bfloat16 [1, 2048, 2048], P(None, 'dp', 'tensor'), may hold values from -0.125 to 0.125
- key_weight: bfloat16 [1, 2048, 1024], P(None, 'dp', 'tensor'), may hold values from -0.125 to 0.125
- value_weight: bfloat16 [1, 2048, 1024], P(None, 'dp', 'tensor'), may hold values from -0.125 to 0.125
- w_out: bfloat16 [1, 2048, 2048], P(None, 'dp', 'tensor'), may hold values from -1 to 1
- w_gate: bfloat16 [1, 2048, 6144], P(None, 'dp', 'tensor'), may hold values from -0.125 to 0.125
- w_up: bfloat16 [1, 2048, 6144], P(None, 'dp', 'tensor'), may hold values from -0.125 to 0.125
- w_down: bfloat16 [1, 2048, 6144], P(None, 'dp', 'tensor'), may hold values from -0.078125 to 0.078125
- gain_in: float32 [1, 2048], replicated, may hold values from 0.5 to 1.5
- gain_post: float32 [1, 2048], replicated, may hold values from 0.5 to 1.5
- gain_query: float32 [1, 128], replicated, may hold values from 0.5 to 1.5
- gain_key: float32 [1, 128], replicated, may hold values from 0.5 to 1.5
- cotangent: bfloat16 [4096, 2048], P(('dp', 'tensor')), may hold values from -6 to 6
Outputs:
- output: bfloat16 [4096, 2048], P(('dp', 'tensor'))
- grad_tokens: bfloat16 [4096, 2048], P(('dp', 'tensor'))
- grad_w_query: float32 [1, 2048, 2048], P(None, 'dp', 'tensor')
- grad_w_key: float32 [1, 2048, 1024], P(None, 'dp', 'tensor')
- grad_w_value: float32 [1, 2048, 1024], P(None, 'dp', 'tensor')
- grad_w_out: float32 [1, 2048, 2048], P(None, 'dp', 'tensor')
- grad_w_gate: float32 [1, 2048, 6144], P(None, 'dp', 'tensor')
- grad_w_up: float32 [1, 2048, 6144], P(None, 'dp', 'tensor')
- grad_w_down: float32 [1, 2048, 6144], P(None, 'dp', 'tensor')
- grad_gain_in: float32 [1, 2048], replicated
- grad_gain_post: float32 [1, 2048], replicated
- grad_gain_query: float32 [1, 128], replicated
- grad_gain_key: float32 [1, 128], replicated
The draws below stay inside these ranges and needn't reach their ends.
Inputs may be any that keep to these rules, and one draw needn't show every extreme that they name: The sequence of group g is its first lengths[g] slots; some group's sequence fills all 512 slots.
All inputs are finite; a program needn't handle non-finite values.
Results may differ from the reference program's by a relative error of at most 0.019.
Values may be sent and summed in bfloat16 or wider, within the bound.
No kernel may reach another device: no remote copies, remote signals or barrier semaphores. Data moves between devices by JAX's collectives and lax.ppermute only.
A program may use at most 128 MiB of HBM per device.

```python
import jax
import jax.numpy as jnp
from jax import lax

MODEL_WIDTH = 2048
QUERY_HEADS = 16
KEY_VALUE_HEADS = 8
HEAD_SIZE = 128
FF = 6144
DECODER_LAYERS = 1
GROUP = 512
NSEQ = 8
TOKENS = 4096


def draw_lengths(key, part):
    drawn = jax.random.randint(jax.random.fold_in(key, 11), (NSEQ,), GROUP // 2, GROUP + 1)
    chosen = jax.random.randint(jax.random.fold_in(key, 12), (), 0, NSEQ)
    return jnp.where(jnp.arange(NSEQ) == chosen, GROUP, drawn).astype(jnp.int32)


def steps_of(key, extent, cuts, least, largest):
    def one(axis_at, shards_of):
        steps = jax.random.uniform(jax.random.fold_in(jax.random.fold_in(key, 6), axis_at), (shards_of,), jnp.float32, least / len(cuts), largest / len(cuts))
        return jnp.repeat(jnp.exp(steps), extent[axis_at] // shards_of).reshape((-1,) + (1,) * (len(extent) - axis_at - 1))

    loudness = one(*cuts[0])
    for cut in cuts[1:]:
        loudness = loudness * one(*cut)
    return loudness


def noise(stream_key, extent, deviation, bound, shards=(), kind=jnp.bfloat16):
    values = jax.random.normal(stream_key, extent, jnp.float32) * deviation
    if len(shards) > 0:
        values = steps_of(stream_key, extent, shards, -0.22, 0.18) * values
    return jnp.clip(values, min=-bound, max=bound).astype(kind)


def setup_inputs(seed: int = 0) -> dict:
    splits = jax.random.split(jax.random.key(seed), 15)
    tokens = noise(splits[0], (TOKENS, MODEL_WIDTH), 1.0, 6.0, ((0, 32),))
    lengths = draw_lengths(jax.random.fold_in(splits[14], 71), 0)
    w_query = noise(splits[2], (DECODER_LAYERS, MODEL_WIDTH, QUERY_HEADS * HEAD_SIZE), MODEL_WIDTH ** -0.5, 0.125, ((1, 8), (2, 4)))
    key_weight = noise(splits[3], (DECODER_LAYERS, MODEL_WIDTH, KEY_VALUE_HEADS * HEAD_SIZE), MODEL_WIDTH ** -0.5, 0.125, ((1, 8), (2, 4)))
    value_weight = noise(splits[4], (DECODER_LAYERS, MODEL_WIDTH, KEY_VALUE_HEADS * HEAD_SIZE), MODEL_WIDTH ** -0.5, 0.125, ((1, 8), (2, 4)))
    w_out = noise(splits[5], (DECODER_LAYERS, MODEL_WIDTH, QUERY_HEADS * HEAD_SIZE), (HEAD_SIZE // 4) ** -0.5, 1.0, ((1, 8), (2, 4)))
    w_gate = noise(splits[6], (DECODER_LAYERS, MODEL_WIDTH, FF), MODEL_WIDTH ** -0.5, 0.125, ((1, 8), (2, 4)))
    w_up = noise(splits[7], (DECODER_LAYERS, MODEL_WIDTH, FF), MODEL_WIDTH ** -0.5, 0.125, ((1, 8), (2, 4)))
    w_down = noise(splits[8], (DECODER_LAYERS, MODEL_WIDTH, FF), FF ** -0.5, 0.078125, ((1, 8), (2, 4)))
    gain_in = jnp.clip(1.0 + 0.1 * jax.random.normal(splits[9], (DECODER_LAYERS, MODEL_WIDTH), jnp.float32), 0.5, 1.5)
    gain_post = jnp.clip(1.0 + 0.1 * jax.random.normal(splits[10], (DECODER_LAYERS, MODEL_WIDTH), jnp.float32), 0.5, 1.5)
    gain_query = jnp.clip(1.0 + 0.1 * jax.random.normal(splits[11], (DECODER_LAYERS, HEAD_SIZE), jnp.float32), 0.5, 1.5)
    gain_key = jnp.clip(1.0 + 0.1 * jax.random.normal(splits[12], (DECODER_LAYERS, HEAD_SIZE), jnp.float32), 0.5, 1.5)
    cotangent = noise(splits[13], (TOKENS, MODEL_WIDTH), 1.0, 6.0, ((0, 32),))
    return {"tokens": tokens, "lengths": lengths, "w_query": w_query, "key_weight": key_weight, "value_weight": value_weight, "w_out": w_out, "w_gate": w_gate, "w_up": w_up, "w_down": w_down, "gain_in": gain_in, "gain_post": gain_post, "gain_query": gain_query, "gain_key": gain_key, "cotangent": cotangent}


@jax.custom_vjp
def reduced_copy(v):
    return lax.optimization_barrier(v.astype(jnp.bfloat16)).astype(jnp.float32)

@jax.custom_vjp
def reduced_backward(v):
    return v

def low_keep(v):
    return (reduced_copy(v), None)

def low_pass(kept, grad):
    return (grad,)

def back_keep(v):
    return (v, None)

def back_low(kept, grad):
    return (reduced_copy(grad),)
reduced_copy.defvjp(low_keep, low_pass)
reduced_backward.defvjp(back_keep, back_low)
EPSILON = 1e-06
THETA = 1000000.0
TOP_PRECISION = lax.Precision.HIGHEST
MASKED = -1e+30

def rms_norm(values, gain):
    return values * lax.rsqrt(lax.optimization_barrier(jnp.mean(values * values, axis=-1, keepdims=True)) + EPSILON) * gain

def rope_tables(count_of_rows, head_size):
    half_size = head_size // 2
    counter = jnp.arange(half_size, dtype=jnp.float32)
    frequency = THETA ** (-2.0 * counter / head_size)
    angles = jnp.arange(count_of_rows, dtype=jnp.float32)[:, None] * frequency[None, :]
    cosine_table = jnp.concatenate([jnp.cos(angles), jnp.cos(angles)], axis=-1)
    sine_table = jnp.concatenate([jnp.sin(angles), jnp.sin(angles)], axis=-1)
    return (cosine_table, sine_table)

def rotate(values, cosine_table, sine_table):
    half_size = values.shape[-1] // 2
    turned = jnp.concatenate([-values[..., half_size:], values[..., :half_size]], axis=-1)
    return values * cosine_table[:, None, :] + turned * sine_table[:, None, :]

def group_layer(rows_in, seq_length, layer_weights, layer_gains, cosine_table, sine_table):
    w_query, key_weight, value_weight, w_out, w_gate, w_up, w_down = layer_weights
    gain_in, gain_post, gain_query, gain_key = layer_gains
    count_of_rows = rows_in.shape[0]
    norm_result = reduced_copy(rms_norm(rows_in, gain_in))
    query_raw = reduced_backward(jnp.dot(norm_result, w_query, precision=TOP_PRECISION)).reshape(count_of_rows, QUERY_HEADS, HEAD_SIZE)
    key_unrotated = reduced_backward(jnp.dot(norm_result, key_weight, precision=TOP_PRECISION)).reshape(count_of_rows, KEY_VALUE_HEADS, HEAD_SIZE)
    value_reduced = reduced_copy(reduced_backward(jnp.dot(norm_result, value_weight, precision=TOP_PRECISION))).reshape(count_of_rows, KEY_VALUE_HEADS, HEAD_SIZE)
    query_reduced = reduced_copy(rotate(rms_norm(query_raw, gain_query), cosine_table, sine_table))
    query_reduced = query_reduced.reshape(count_of_rows, KEY_VALUE_HEADS, QUERY_HEADS // KEY_VALUE_HEADS, HEAD_SIZE)
    key_low = reduced_copy(rotate(rms_norm(key_unrotated, gain_key), cosine_table, sine_table))
    scores = reduced_backward(jnp.einsum('qkgd,skd->kgqs', query_reduced, key_low, precision=TOP_PRECISION) * HEAD_SIZE ** (-0.5))
    row_index = lax.broadcasted_iota(jnp.int32, (count_of_rows, count_of_rows), 0)
    column_index = lax.broadcasted_iota(jnp.int32, (count_of_rows, count_of_rows), 1)
    allowed = (column_index <= row_index) & (row_index < seq_length) | (column_index == row_index)
    masked = jnp.where(allowed, scores, MASKED)
    row_max = lax.optimization_barrier(jnp.max(masked, axis=-1, keepdims=True))
    expanded = jnp.exp(masked - row_max)
    probability = reduced_copy(expanded / lax.optimization_barrier(jnp.sum(expanded, axis=-1, keepdims=True)))
    attended = jnp.einsum('kgqs,skd->qkgd', probability, value_reduced, precision=TOP_PRECISION).reshape(count_of_rows, QUERY_HEADS * HEAD_SIZE)
    attended = reduced_copy(reduced_backward(attended))
    middle = rows_in + reduced_backward(jnp.dot(attended, w_out.T, precision=TOP_PRECISION))
    post = reduced_copy(rms_norm(middle, gain_post))
    gate_value = reduced_backward(jnp.dot(post, w_gate, precision=TOP_PRECISION))
    up_value = reduced_backward(jnp.dot(post, w_up, precision=TOP_PRECISION))
    hidden = reduced_copy(jax.nn.silu(gate_value) * up_value)
    return middle + reduced_backward(jnp.dot(hidden, w_down.T, precision=TOP_PRECISION))

def reference(tokens, lengths, w_query, key_weight, value_weight, w_out, w_gate, w_up, w_down, gain_in, gain_post, gain_query, gain_key, cotangent):
    cosine_table, sine_table = rope_tables(GROUP, HEAD_SIZE)
    weight_set = tuple((member.astype(jnp.float32) for member in (w_query, key_weight, value_weight, w_out, w_gate, w_up, w_down)))
    gain_set = (gain_in, gain_post, gain_query, gain_key)

    def forward(inputs, weights_now, gains_now):
        stream = inputs.reshape(NSEQ, GROUP, MODEL_WIDTH)
        for layer_index in range(DECODER_LAYERS):
            layer_weights = tuple((member[layer_index] for member in weights_now))
            layer_gains = tuple((member[layer_index] for member in gains_now))

            def one_group(group_pair, layer_weights=layer_weights, layer_gains=layer_gains):
                return group_layer(group_pair[0], group_pair[1], layer_weights, layer_gains, cosine_table, sine_table)
            stream = lax.map(jax.checkpoint(one_group), (stream, lengths))
        return stream.reshape(TOKENS, MODEL_WIDTH)
    result, pullback = jax.vjp(forward, tokens.astype(jnp.float32), weight_set, gain_set)
    grad_inputs, grad_weights, grad_gains = pullback(cotangent.astype(jnp.float32))
    return (result.astype(jnp.bfloat16), grad_inputs.astype(jnp.bfloat16), grad_weights[0], grad_weights[1], grad_weights[2], grad_weights[3], grad_weights[4], grad_weights[5], grad_weights[6], grad_gains[0], grad_gains[1], grad_gains[2], grad_gains[3])
```

```python
import jax
import jax.numpy as jnp
from jax import lax
from jax.sharding import PartitionSpec as P


QUERY_HEADS = 16
KEY_VALUE_HEADS = 8
HEAD_SIZE = 128

EPSILON = 1e-06
THETA = 1000000.0
MASKED = -1e30


def normalize(values):
    inverse = lax.rsqrt(jnp.mean(values * values, axis=-1, keepdims=True) + EPSILON)
    return (values * inverse, inverse)


def norm_back(gradient, scaled, inverse, gain):
    weighted = gradient * gain
    d_values = inverse * (weighted - scaled * jnp.mean(weighted * scaled, axis=-1, keepdims=True))
    d_gain = jnp.sum((gradient * scaled).reshape(-1, gradient.shape[-1]), axis=0)
    return (d_values, d_gain)


def rope_tables(count_of_rows, head_size):
    half_size = head_size // 2
    counter = jnp.arange(half_size, dtype=jnp.float32)
    frequency = THETA ** (-2.0 * counter / head_size)
    angles = jnp.arange(count_of_rows, dtype=jnp.float32)[:, None] * frequency[None, :]
    cosine_table = jnp.concatenate([jnp.cos(angles), jnp.cos(angles)], axis=-1)
    sine_table = jnp.concatenate([jnp.sin(angles), jnp.sin(angles)], axis=-1)
    return (cosine_table, sine_table)


def rotate(values, cosine_table, sine_table):
    half_size = values.shape[-1] // 2
    turned = jnp.concatenate([-values[..., half_size:], values[..., :half_size]], axis=-1)
    return values * cosine_table[:, None, :] + turned * sine_table[:, None, :]


def unrotate(values, cosine_table, sine_table):
    half_size = values.shape[-1] // 2
    moved = values * sine_table[:, None, :]
    turned = jnp.concatenate([moved[..., half_size:], -moved[..., :half_size]], axis=-1)
    return values * cosine_table[:, None, :] + turned


def block_scores(query_block, keys, first_row, seq_length, score_scale):
    scores = (
        jnp.einsum("qkgd,skd->kgqs", query_block, keys, preferred_element_type=jnp.float32)
        * score_scale
    )
    shape_now = (query_block.shape[0], keys.shape[0])
    row_index = first_row + lax.broadcasted_iota(jnp.int32, shape_now, 0)
    column_index = lax.broadcasted_iota(jnp.int32, shape_now, 1)
    allowed = (column_index <= row_index) & (row_index < seq_length) | (column_index == row_index)
    return jnp.where(allowed, scores, MASKED)


def attend_block(query_block, keys, values, first_row, seq_length, score_scale):
    masked = block_scores(query_block, keys, first_row, seq_length, score_scale)
    row_max = jnp.max(masked, axis=-1, keepdims=True)
    expanded = jnp.exp(masked - row_max)
    row_sum = jnp.sum(expanded, axis=-1, keepdims=True)
    probability = (expanded / row_sum).astype(jnp.bfloat16)
    attended = jnp.einsum("kgqs,skd->qkgd", probability, values, preferred_element_type=jnp.float32)
    return (attended, row_max, row_sum)


def attend_back(
    query_block, keys, values, d_block, row_max, row_sum, first_row, seq_length, score_scale
):
    masked = block_scores(query_block, keys, first_row, seq_length, score_scale)
    probability = jnp.exp(masked - row_max) / row_sum
    d_probability = jnp.einsum(
        "qkgd,skd->kgqs", d_block, values, preferred_element_type=jnp.float32
    )
    centre = jnp.sum(probability * d_probability, axis=-1, keepdims=True)
    d_scores = (probability * (d_probability - centre)).astype(jnp.bfloat16)
    grad_query = (
        jnp.einsum("kgqs,skd->qkgd", d_scores, keys, preferred_element_type=jnp.float32)
        * score_scale
    )
    grad_key = (
        jnp.einsum("kgqs,qkgd->skd", d_scores, query_block, preferred_element_type=jnp.float32)
        * score_scale
    )
    grad_value = jnp.einsum(
        "kgqs,qkgd->skd",
        probability.astype(jnp.bfloat16),
        d_block,
        preferred_element_type=jnp.float32,
    )
    return (grad_query, grad_key, grad_value)


def contract_rows(left, right):
    return lax.dot_general(
        left, right, (((0,), (0,)), ((), ())), preferred_element_type=jnp.float32
    )


def contract_cols(left, right):
    return lax.dot_general(
        left, right, (((1,), (1,)), ((), ())), preferred_element_type=jnp.float32
    )


def send(value, pairs):
    return lax.ppermute(value, "dp", pairs)


class Grid:
    def __init__(self):
        self.count = lax.axis_size("dp")
        self.index = lax.axis_index("dp")
        self.line = self.count // 2
        self.place = self.index // 2
        self.across = [(i, i ^ 1) for i in range(self.count)]

    def steps(self, first, last, move):
        return [(2 * p + s, 2 * (p + move) + s) for p in range(first, last) for s in range(2)]

    def relative(self, values):
        width = values.shape[-1] // self.count
        blocks = [values[..., k * width : (k + 1) * width] for k in range(self.count)]
        bit = 1
        while bit < self.count:
            on = (self.index & bit) != 0
            blocks = [jnp.where(on, blocks[k ^ bit], blocks[k]) for k in range(self.count)]
            bit *= 2
        return jnp.concatenate(blocks, axis=-1)

    def gather(self, shard):
        up = self.steps(0, self.line - 1, 1)
        down = self.steps(1, self.line, -1)
        left, right = ([shard], [shard])
        blocks = [shard, send(shard, self.across)]
        for r in range(1, self.line):
            left.append(send(left[-1], up))
            right.append(send(right[-1], down))
            seen_left, seen_right = (list(left), list(right))
            if r > 1:
                tied = lax.optimization_barrier(tuple(left[1:] + right[1:]))
                seen_left[1:], seen_right[1:] = (list(tied[:r]), list(tied[r:]))
            target = self.place ^ r
            block = None
            for d in range(1, r + 1):
                if (d ^ r) & 1:
                    continue
                for hit, piece in (
                    (target == self.place - d, seen_left[d]),
                    (target == self.place + d, seen_right[d]),
                ):
                    block = piece if block is None else jnp.where(hit, piece, block)
            blocks += [block, send(block, self.across)]
        return jnp.concatenate(blocks, axis=0)

    def scatter_sum(self, part):
        halves = {}
        for r in reversed(range(self.line)):
            other = send(part(2 * r + 1).astype(jnp.bfloat16), self.across)
            halves[r] = (part(2 * r) + other.astype(jnp.float32)).astype(jnp.bfloat16)
        up = down = None
        for s in range(1, self.line):
            up_pick = down_pick = None
            for p in range(s):
                up_from = halves[p ^ (p + self.line - s)]
                up_pick = up_from if up_pick is None else jnp.where(self.place == p, up_from, up_pick)
                q = self.line - 1 - p
                down_from = halves[q ^ (q - self.line + s)]
                down_pick = (
                    down_from if down_pick is None else jnp.where(self.place == q, down_from, down_pick)
                )
            if up is not None:
                up_pick = (up_pick.astype(jnp.float32) + up.astype(jnp.float32)).astype(jnp.bfloat16)
                down_pick = (down_pick.astype(jnp.float32) + down.astype(jnp.float32)).astype(jnp.bfloat16)
            up = send(up_pick, self.steps(0, s, 1))
            down = send(down_pick, self.steps(self.line - s, self.line, -1))
        total = halves[0].astype(jnp.float32)
        if up is not None:
            total = total + up.astype(jnp.float32) + down.astype(jnp.float32)
        return total


def gather_rows(values):
    return lax.all_gather(values, "tensor", axis=0, tiled=True)


def scatter_rows(values):
    return lax.psum_scatter(values, "tensor", scatter_dimension=0, tiled=True).astype(jnp.float32)


def layer(
    tokens,
    lengths,
    w_query,
    key_weight,
    value_weight,
    w_out,
    w_gate,
    w_up,
    w_down,
    gain_in,
    gain_post,
    gain_query,
    gain_key,
    cotangent,
):
    tensor_shard_count = lax.axis_size("tensor")
    group_rows = tokens.shape[0] * tensor_shard_count
    seq_length = lengths[0]
    score_scale = HEAD_SIZE ** (-0.5)
    query_heads = QUERY_HEADS // tensor_shard_count
    key_value_heads = KEY_VALUE_HEADS // tensor_shard_count
    heads_per_group = QUERY_HEADS // KEY_VALUE_HEADS
    query_width = query_heads * HEAD_SIZE
    key_width = key_value_heads * HEAD_SIZE
    units = w_gate.shape[2]
    grid = Grid()
    block_width = tokens.shape[1] // grid.count
    cosine_table, sine_table = rope_tables(group_rows, HEAD_SIZE)

    def columns(values, k):
        return values[:, k * block_width : (k + 1) * block_width]

    weights_in = grid.gather(jnp.concatenate([w_query[0], key_weight[0], value_weight[0]], axis=1))
    weights_out = grid.gather(w_out[0])
    weights_up = grid.gather(jnp.concatenate([w_gate[0], w_up[0]], axis=1))
    weights_down = grid.gather(w_down[0])

    gain_first = grid.relative(gain_in[0])
    gain_second = grid.relative(gain_post[0])

    gradient_low = grid.relative(cotangent)
    d_mlp = gather_rows(gradient_low)
    gradient = gradient_low.astype(jnp.float32)

    stream = grid.relative(tokens).astype(jnp.float32)
    scaled_in, inverse_in = normalize(stream)
    normed_rows = gather_rows((scaled_in * gain_first).astype(jnp.bfloat16))
    projected = jnp.dot(normed_rows, weights_in, preferred_element_type=jnp.float32)
    query_raw = projected[:, :query_width].reshape(group_rows, query_heads, HEAD_SIZE)
    key_raw = projected[:, query_width : query_width + key_width].reshape(
        group_rows, key_value_heads, HEAD_SIZE
    )
    value_low = (
        projected[:, query_width + key_width :]
        .astype(jnp.bfloat16)
        .reshape(group_rows, key_value_heads, HEAD_SIZE)
    )
    query_hat, query_inverse = normalize(query_raw)
    query_low = rotate(query_hat * gain_query[0], cosine_table, sine_table).astype(jnp.bfloat16)
    query_low = query_low.reshape(group_rows, key_value_heads, heads_per_group, HEAD_SIZE)
    key_hat, key_inverse = normalize(key_raw)
    key_low = rotate(key_hat * gain_key[0], cosine_table, sine_table).astype(jnp.bfloat16)
    attended, row_max, row_sum = attend_block(
        query_low, key_low, value_low, 0, seq_length, score_scale
    )
    attended_low = attended.reshape(group_rows, query_width).astype(jnp.bfloat16)
    middle = stream + scatter_rows(contract_cols(attended_low, weights_out))
    scaled_post, inverse_post = normalize(middle)
    post_rows = gather_rows((scaled_post * gain_second).astype(jnp.bfloat16))
    gate_up = jnp.dot(post_rows, weights_up, preferred_element_type=jnp.float32)
    gate_value, up_value = (gate_up[:, :units], gate_up[:, units:])
    hidden_low = (jax.nn.silu(gate_value) * up_value).astype(jnp.bfloat16)
    grad_down = grid.scatter_sum(lambda k: contract_rows(columns(d_mlp, k), hidden_low))
    output = middle + scatter_rows(contract_cols(hidden_low, weights_down).astype(jnp.bfloat16))

    d_hidden = jnp.dot(d_mlp, weights_down, preferred_element_type=jnp.float32)
    sigmoid_gate = jax.nn.sigmoid(gate_value)
    d_gate = (
        d_hidden * up_value * sigmoid_gate * (1.0 + gate_value * (1.0 - sigmoid_gate))
    ).astype(jnp.bfloat16)
    d_up = (d_hidden * gate_value * sigmoid_gate).astype(jnp.bfloat16)
    d_gate_up = jnp.concatenate([d_gate, d_up], axis=1)
    grad_gate_up = grid.scatter_sum(lambda k: contract_rows(columns(post_rows, k), d_gate_up))
    d_post = scatter_rows(contract_cols(d_gate_up, weights_up).astype(jnp.bfloat16))
    d_middle_norm, grad_post_gain = norm_back(d_post, scaled_post, inverse_post, gain_second)
    d_middle = gradient + d_middle_norm
    d_attn = gather_rows(d_middle.astype(jnp.bfloat16))
    grad_out = grid.scatter_sum(lambda k: contract_rows(columns(d_attn, k), attended_low))
    d_attended = jnp.dot(d_attn, weights_out, preferred_element_type=jnp.float32).astype(
        jnp.bfloat16
    )
    d_attended = d_attended.reshape(group_rows, key_value_heads, heads_per_group, HEAD_SIZE)
    d_query, d_key, d_value = attend_back(
        query_low, key_low, value_low, d_attended, row_max, row_sum, 0, seq_length, score_scale
    )
    d_query_hat = unrotate(
        d_query.reshape(group_rows, query_heads, HEAD_SIZE), cosine_table, sine_table
    )
    d_query_raw, grad_query_gain = norm_back(d_query_hat, query_hat, query_inverse, gain_query[0])
    d_key_hat = unrotate(d_key, cosine_table, sine_table)
    d_key_raw, grad_key_gain = norm_back(d_key_hat, key_hat, key_inverse, gain_key[0])
    d_projected = jnp.concatenate(
        [
            d_query_raw.reshape(group_rows, query_width),
            d_key_raw.reshape(group_rows, key_width),
            d_value.reshape(group_rows, key_width),
        ],
        axis=1,
    ).astype(jnp.bfloat16)
    grad_in = grid.scatter_sum(lambda k: contract_rows(columns(normed_rows, k), d_projected))
    d_normed = scatter_rows(contract_cols(d_projected, weights_in).astype(jnp.bfloat16))
    d_stream_norm, grad_in_gain = norm_back(d_normed, scaled_in, inverse_in, gain_first)
    gradient = d_middle + d_stream_norm
    gains = (
        grid.relative(grad_in_gain)[None],
        grid.relative(grad_post_gain)[None],
        grad_query_gain[None],
        grad_key_gain[None],
    )
    gain_totals = lax.psum(gains, ("dp", "tensor"))
    return (
        grid.relative(output.astype(jnp.bfloat16)),
        grid.relative(gradient.astype(jnp.bfloat16)),
        grad_in[None, :, :query_width],
        grad_in[None, :, query_width : query_width + key_width],
        grad_in[None, :, query_width + key_width :],
        grad_out[None],
        grad_gate_up[None, :, :units],
        grad_gate_up[None, :, units:],
        grad_down[None],
    ) + tuple(gain_totals)


def solution(mesh):
    weight = P(None, "dp", "tensor")
    rows = P(("dp", "tensor"), None)
    return jax.shard_map(
        layer,
        mesh=mesh,
        in_specs=(rows, P("dp")) + (weight,) * 7 + (P(),) * 4 + (rows,),
        out_specs=(rows, rows) + (weight,) * 7 + (P(),) * 4,
        check_vma=False,
    )
```
